512 devices in a mesh: tile: 64 (over z, y), rx: 8 (over x, core).
Axes of the slice: x: 4, y: 4, z: 16, core: 2. Of those that a mesh axis runs over, the one named last changes fastest.
Arguments:
- h_adjoint: bfloat16 [128, 2, 3, 64, 64, 128], P('rx', None, None, 'tile'), may hold values from -6 to 6
- conductivity: float32 [64, 64, 128], P(None, 'tile'), may hold values from 0.5 to 5
- tx_field: bfloat16 [128, 2, 3, 64, 64, 128], P('rx', None, None, None, 'tile'), may hold values from -6 to 6
- data_weight: float32 [128, 128], P('rx'), may hold values from -1.5 to 1.5
- tow_index: int32 [8, 8, 2], replicated, may hold values from 0 to 15, as said below
- tow_count: int32 [8, 8], replicated, may hold values from 0 to 2, as said below
Outputs:
- jacobian: float32 [128, 64, 64, 128], P('rx', None, 'tile')
The draws below stay inside these ranges and needn't reach their ends.
Inputs may be any that keep to these rules, and one draw needn't show every extreme that they name: Each block lists consecutive receivers: tow_index[s, d, j] = tow_index[s, d, 0] + j; slots j >= tow_count[s, d] are padding that no output reads. `tow_count`: in every draw some transmitter group has 2 used slots from every receiver group.
All inputs are finite; a program needn't handle non-finite values.
Results may differ from the reference program's by a relative error of at most 0.0041.
Values may be sent and summed in bfloat16 or wider, within the bound.
A program may use at most 128 MiB of HBM per device.

```python
import math
import jax
import jax.numpy as jnp
from jax import lax

NY = 128
TX_DEV = 16
RX_DEV = 16
CAP = 2
OWNERS = 8
NX = 64
NZ = 64
RECV = 128
TX = 128


def draw_tow_index(key, part):
    start_key, first_key, second_key = jax.random.split(key, 3)
    blocks = OWNERS * OWNERS
    starts = jax.random.randint(start_key, (blocks,), 0, RX_DEV - CAP + 1)
    low_at = jax.random.randint(first_key, (), 0, blocks)
    high_at = (low_at + 1 + jax.random.randint(second_key, (), 0, blocks - 1)) % blocks
    places = jnp.arange(blocks)
    starts = jnp.where(places == low_at, 0, starts)
    starts = jnp.where(places == high_at, RX_DEV - CAP, starts)
    listing = starts[:, None] + jnp.arange(CAP)[None, :]
    return listing.reshape(OWNERS, OWNERS, CAP).astype(jnp.int32)


def draw_tow_count(key, part):
    base_key, column_key, row_key = jax.random.split(key, 3)
    counts = jax.random.randint(base_key, (OWNERS, OWNERS), 0, CAP + 1)
    full_column = jax.random.randint(column_key, (), 0, OWNERS)
    empty_row = jax.random.randint(row_key, (), 0, OWNERS)
    columns = jnp.arange(OWNERS)[None, :]
    row_places = jnp.arange(OWNERS)[:, None]
    counts = jnp.where(columns == full_column, CAP, counts)
    counts = jnp.where((columns == (full_column + 1) % OWNERS) & (row_places == empty_row), 0, counts)
    return counts.astype(jnp.int32)


def block_scale(own_key, extent, cuts, low, high):
    factor_of, own = 1.0, jax.random.fold_in(own_key, 6)
    for axis_at, shards_of in cuts:
        heights = jnp.exp(jax.random.uniform(jax.random.fold_in(own, axis_at), (shards_of,), jnp.float32, low / len(cuts), high / len(cuts)))
        factor_of = factor_of * jnp.repeat(heights, extent[axis_at] // shards_of).reshape([-1 if axis == axis_at else 1 for axis in range(len(extent))])
    return factor_of


def normal_values(rng, dims, scale, reach, shards=(), kind=jnp.bfloat16):
    entries = scale * jax.random.normal(rng, dims, jnp.float32)
    if shards:
        entries = entries * block_scale(rng, dims, shards, -0.22, 0.18)
    return jnp.clip(entries, -reach, reach).astype(kind)


def setup_inputs(seed: int = 0) -> dict:
    arg_keys = jax.random.split(jax.random.key(seed), 7)
    h_adjoint = normal_values(arg_keys[0], (RECV, 2, 3, NX, NZ, NY), 1.0, 6.0, ((0, 8), (3, 64)))
    conductivity = jnp.clip(jnp.exp(math.log(5.0) - 2.3025851 * jax.random.uniform(arg_keys[1], (NX, NZ, NY), jnp.float32) ** block_scale(arg_keys[1], (NX, NZ, NY), ((1, 64),), -0.2, 0.2)), 0.5, 5.0)
    tx_field = normal_values(arg_keys[2], (TX, 2, 3, NX, NZ, NY), 1.0, 6.0, ((0, 8), (4, 64)))
    data_weight = normal_values(arg_keys[3], (TX, RECV), (OWNERS * CAP) ** -0.5, 1.5, ((0, 8),), jnp.float32)
    tow_index = draw_tow_index(jax.random.fold_in(arg_keys[6], 71), 0)
    tow_count = draw_tow_count(jax.random.fold_in(arg_keys[6], 71), 0)
    return dict(h_adjoint=h_adjoint, conductivity=conductivity, tx_field=tx_field, data_weight=data_weight, tow_index=tow_index, tow_count=tow_count)


def lagged(values, along):
    along = along % values.ndim
    length = values.shape[along]
    border = jnp.zeros_like(lax.slice_in_dim(values, 0, 1, axis=along))
    return jnp.concatenate([border, lax.slice_in_dim(values, 0, length - 1, axis=along)], axis=along)


def curl_average(potential):
    field_x = potential[..., 0, :, :, :]
    field_y = potential[..., 1, :, :, :]
    field_z = potential[..., 2, :, :, :]
    curl_x = (field_z - lagged(field_z, -1)) - (field_y - lagged(field_y, -2))
    curl_y = (field_x - lagged(field_x, -2)) - (field_z - lagged(field_z, -3))
    curl_z = (field_y - lagged(field_y, -3)) - (field_x - lagged(field_x, -1))
    average_x = 0.5 * (curl_x + lagged(curl_x, -3))
    average_y = 0.5 * (curl_y + lagged(curl_y, -1))
    average_z = 0.5 * (curl_z + lagged(curl_z, -2))
    return jnp.stack([average_x, average_y, average_z], axis=-4)


def reference(h_adjoint, conductivity, tx_field, data_weight, tow_index, tow_count):
    def per_receiver(potential):
        return (curl_average(potential.astype(jnp.float32)) / conductivity).astype(jnp.bfloat16)

    cell_fields = lax.map(per_receiver, h_adjoint)
    slot_ids = jnp.arange(CAP, dtype=jnp.int32)
    in_use = (slot_ids[None, None, :] < tow_count[:, :, None]).astype(jnp.float32)
    matches = (tow_index[..., None] == jnp.arange(RX_DEV, dtype=jnp.int32)).astype(jnp.float32) * in_use[..., None]
    listed = jnp.transpose(jnp.sum(matches, axis=2), (1, 0, 2)).reshape(OWNERS, RECV)
    coupling = (data_weight * jnp.repeat(listed, TX_DEV, axis=0)).astype(jnp.bfloat16)
    coupling = lax.optimization_barrier(coupling).astype(jnp.float32)

    def per_layer(layer):
        layer_field = lax.dynamic_index_in_dim(cell_fields, layer, axis=4, keepdims=False).astype(jnp.float32)
        source = lax.dynamic_index_in_dim(tx_field, layer, axis=4, keepdims=False).astype(jnp.float32)
        combined = jnp.einsum("tq,qpcxy->tpcxy", coupling, layer_field)
        return jnp.sum(combined[:, 0] * source[:, 0] - combined[:, 1] * source[:, 1], axis=1)

    layers = lax.map(per_layer, jnp.arange(NZ, dtype=jnp.int32))
    return jnp.transpose(layers, (1, 2, 0, 3))
```

```python
import functools

import jax
import jax.numpy as jnp
from jax import lax
from jax.experimental import pallas as pl
from jax.experimental.pallas import tpu as pltpu
from jax.sharding import PartitionSpec as P

XG = 8
RU = 4
MESH = pl.DeviceIdType.MESH


def group_order(groups):
    far = groups // 2
    order = [far]
    for step in range(1, groups):
        for offset in (far - step, far + step):
            if 0 < offset < groups and offset not in order:
                order.append(offset)
    if 0 not in order:
        order.append(0)
    return order


def kernel(messages, h_ref, tx_ref, sigma_ref, sel_ref, coef_ref, out_ref,
           halo, sent, arrived, picked, fields, halo_send, halo_recv,
           tile_send, tile_recv, rx_send, rx_recv):
    tiles = lax.axis_size("tile")
    owners = lax.axis_size("rx")
    me = lax.axis_index("tile")
    own = lax.axis_index("rx")
    groups = tiles // XG
    order = group_order(groups)
    my_group = me // XG
    units = h_ref.shape[0]
    after = lax.rem(me + 1, tiles)

    barrier = pltpu.get_barrier_semaphore()

    def greet_tile(step, _):
        peer = lax.rem(me + step, tiles)
        pl.semaphore_signal(barrier, inc=1, device_id={"tile": peer}, device_id_type=MESH)
        return 0

    def greet_rx(step, _):
        peer = lax.rem(own + step, owners)
        pl.semaphore_signal(barrier, inc=1, device_id={"rx": peer}, device_id_type=MESH)
        return 0

    lax.fori_loop(1, tiles, greet_tile, 0)
    lax.fori_loop(1, owners, greet_rx, 0)
    pl.semaphore_wait(barrier, tiles + owners - 2)

    def halo_copy(unit):
        return pltpu.make_async_remote_copy(
            src_ref=h_ref.at[unit, pl.ds(1, 2)], dst_ref=halo.at[unit],
            send_sem=halo_send.at[unit], recv_sem=halo_recv.at[unit],
            device_id={"tile": after}, device_id_type=MESH)

    for unit in range(units):
        halo_copy(unit).start()

    inner = (me > 0).astype(jnp.float32)
    lanes = lax.broadcasted_iota(jnp.int32, (XG, 8, 128), 2)

    def lag_y(value):
        return jnp.where(lanes == 0, 0.0, pltpu.roll(value, 1, 2))

    def curl_block(unit, base):
        hx = h_ref[unit, 0, pl.ds(base, XG + 1)].astype(jnp.float32)
        hy = h_ref[unit, 1, pl.ds(base, XG + 1)].astype(jnp.float32)
        hz = h_ref[unit, 2, pl.ds(base + 1, XG)].astype(jnp.float32)
        py = halo[unit, 0, pl.ds(base, XG + 1)].astype(jnp.float32) * inner
        pz = halo[unit, 1, pl.ds(base + 1, XG)].astype(jnp.float32) * inner
        both_y = hy + py
        both_z = hz + pz
        diff_xy = hy - py
        curl_y = (hx[1:] - hx[:-1]) - (hz - pz)
        sum_x = hx[1:] + hx[:-1]
        average_x = 0.5 * ((both_z - lag_y(both_z)) - (both_y[1:] - both_y[:-1]))
        average_y = 0.5 * (curl_y + lag_y(curl_y))
        average_z = 0.5 * ((diff_xy[1:] + diff_xy[:-1]) - (sum_x - lag_y(sum_x)))
        sent[pl.ds(base, XG), unit, 0] = average_x.astype(jnp.bfloat16)
        sent[pl.ds(base, XG), unit, 1] = average_y.astype(jnp.bfloat16)
        sent[pl.ds(base, XG), unit, 2] = average_z.astype(jnp.bfloat16)

    first = 0
    for number, count in enumerate(messages):
        span = pl.ds(first, count)
        for unit in range(first, first + count):
            halo_copy(unit).wait_recv()
        for offset in order:
            base = lax.rem(my_group + offset, groups) * XG
            for unit in range(first, first + count):
                curl_block(unit, base)

            def send(step, _, base=base, span=span, number=number):
                layer = base + step

                @pl.when(layer != me)
                def _():
                    pltpu.make_async_remote_copy(
                        src_ref=sent.at[layer, span], dst_ref=arrived.at[me, span],
                        send_sem=tile_send.at[number],
                        recv_sem=tile_recv.at[number, my_group],
                        device_id={"tile": layer}, device_id_type=MESH).start()

                @pl.when(layer == me)
                def _():
                    pltpu.make_async_copy(
                        sent.at[layer, span], arrived.at[me, span],
                        tile_recv.at[number, my_group]).start()
                return 0

            lax.fori_loop(0, XG, send, 0)
        first += count

    def collect(offset):
        group = lax.rem(my_group + groups - offset, groups)
        first = 0
        for number, count in enumerate(messages):
            whole = arrived.at[pl.ds(group * XG, XG), pl.ds(first, count)]
            pltpu.make_async_copy(whole, whole, tile_recv.at[number, group]).wait()
            first += count
        for part in range(3):
            block = arrived[pl.ds(group * XG, XG), :, part]
            block = block.reshape(XG * units * 8, 128)
            chosen = jnp.dot(sel_ref[...], block, preferred_element_type=jnp.float32)
            picked[group, :, part] = chosen.astype(jnp.bfloat16).reshape(owners, 4 * XG, 128)
        fields[group, own] = picked[group, own]

        def forward(step, _):
            peer = lax.rem(own + step, owners)
            pltpu.make_async_remote_copy(
                src_ref=picked.at[group, peer], dst_ref=fields.at[group, own],
                send_sem=rx_send, recv_sem=rx_recv.at[group],
                device_id={"rx": peer}, device_id_type=MESH).start()
            return 0

        lax.fori_loop(1, owners, forward, 0)

    def finish(offset):
        group = lax.rem(my_group + groups - offset, groups)
        others = fields.at[group, pl.ds(0, owners - 1)]
        pltpu.make_async_copy(others, others, rx_recv.at[group]).wait()
        total = None
        for part in range(3):
            block = fields[group, :, part].reshape(owners * 4 * XG, 128)
            combined = jnp.dot(coef_ref[...], block, preferred_element_type=jnp.float32)
            term = combined * tx_ref[group, part].astype(jnp.float32)
            total = term if total is None else total + term
        total = total.reshape(XG, 2, out_ref.shape[2], 128)
        value = total[:, 0] - total[:, 1]
        out_ref[group] = value / sigma_ref[group][:, None, :]

    behind = 2 if groups > 2 else 1
    for place, offset in enumerate(order):
        collect(offset)
        if place >= behind:
            finish(order[place - behind])
    for offset in order[len(order) - min(behind, len(order)):]:
        finish(offset)

    for unit in range(units):
        halo_copy(unit).wait_send()
    first = 0
    for number, count in enumerate(messages):
        rest = sent.at[pl.ds(0, tiles - 1), pl.ds(first, count)]
        pltpu.make_async_copy(rest, rest, tile_send.at[number]).wait()
        first += count
    rest = picked.at[:, pl.ds(0, owners - 1)]
    pltpu.make_async_copy(rest, rest, rx_send).wait()


def transfer(h_units, tx_groups, sigma_groups, sel, coef, messages, call_id):
    units = h_units.shape[0]
    groups, _, rows, cells_y = tx_groups.shape
    tiles = groups * XG
    owners = sel.shape[0] // (4 * XG)
    sources = rows // (2 * XG)
    vmem = pl.BlockSpec(memory_space=pltpu.VMEM)
    bf16 = jnp.bfloat16
    return pl.pallas_call(
        functools.partial(kernel, messages),
        out_shape=jax.ShapeDtypeStruct((groups, XG, sources, cells_y), jnp.float32),
        in_specs=[vmem] * 5,
        out_specs=vmem,
        scratch_shapes=[
            pltpu.VMEM((units, 2, tiles + 1, 8, cells_y), bf16),
            pltpu.VMEM((tiles, units, 3, 8, cells_y), bf16),
            pltpu.VMEM((tiles, units, 3, 8, cells_y), bf16),
            pltpu.VMEM((groups, owners, 3, 4 * XG, cells_y), bf16),
            pltpu.VMEM((groups, owners, 3, 4 * XG, cells_y), bf16),
            pltpu.SemaphoreType.DMA((units,)),
            pltpu.SemaphoreType.DMA((units,)),
            pltpu.SemaphoreType.DMA((len(messages),)),
            pltpu.SemaphoreType.DMA((len(messages), groups)),
            pltpu.SemaphoreType.DMA,
            pltpu.SemaphoreType.DMA((groups,)),
        ],
        compiler_params=pltpu.CompilerParams(
            collective_id=call_id, has_side_effects=True, vmem_limit_bytes=40 * 1024 * 1024),
    )(h_units, tx_groups, sigma_groups, sel, coef)


def on_device(h_adjoint, conductivity, tx_field, data_weight, tow_index, tow_count):
    owners = lax.axis_size("rx")
    own = lax.axis_index("rx")
    receivers, parts, axes, _, layers, cells_y = h_adjoint.shape
    sources = tx_field.shape[0]
    capacity = tow_index.shape[2]
    groups = layers // XG
    units = receivers // RU

    h_units = h_adjoint.reshape(units, RU, parts, axes, layers, cells_y)
    h_units = jnp.transpose(h_units, (0, 3, 4, 2, 1, 5))
    h_units = h_units.reshape(units, axes, layers, parts * RU, cells_y)
    h_units = jnp.pad(h_units, ((0, 0), (0, 0), (1, 0), (0, 0), (0, 0)))

    tx_groups = tx_field.reshape(sources, parts, axes, groups, XG, cells_y)
    tx_groups = jnp.transpose(tx_groups, (3, 2, 4, 1, 0, 5))
    tx_groups = tx_groups.reshape(groups, axes, XG * parts * sources, cells_y)
    sigma_groups = conductivity.reshape(groups, XG, cells_y)

    slots = jnp.arange(capacity, dtype=jnp.int32)
    listed = lax.dynamic_index_in_dim(tow_index, own, 0, False)
    same_x = jnp.arange(XG)[:, None] == jnp.arange(XG)[None, :]
    same_part = jnp.arange(parts)[:, None] == jnp.arange(parts)[None, :]
    number = jnp.arange(receivers, dtype=jnp.int32).reshape(units, RU)
    sel = (
        same_x[None, :, None, None, :, None, None, None]
        & same_part[None, None, :, None, None, None, :, None]
        & (listed[:, None, None, :, None, None, None, None]
           == number[None, None, None, None, None, :, None, :])
    )
    sel = sel.astype(jnp.bfloat16).reshape(owners * XG * parts * capacity, XG * units * parts * RU)

    indices_in = lax.dynamic_index_in_dim(tow_index, own, 1, False)
    counts_in = lax.dynamic_index_in_dim(tow_count, own, 1, False)
    in_use = slots[None, :] < counts_in[:, None]
    target = jnp.arange(owners, dtype=jnp.int32)[:, None] * receivers + indices_in
    chosen = (target[:, :, None] == jnp.arange(receivers * owners, dtype=jnp.int32)) & in_use[:, :, None]
    coupling = jnp.sum(
        jnp.where(chosen[None], data_weight[:, None, None, :], 0.0), axis=-1
    ).astype(jnp.bfloat16)
    coef = jnp.where(
        same_x[:, None, None, None, :, None, None]
        & same_part[None, :, None, None, None, :, None],
        coupling[None, None, :, :, None, None, :],
        jnp.zeros((), jnp.bfloat16),
    ).reshape(XG * parts * sources, owners * XG * parts * capacity)

    messages = (1, units - 1)
    rows = transfer(h_units, tx_groups, sigma_groups, sel, coef, messages, 0)
    rows = rows.reshape(layers, sources, cells_y)
    return jnp.transpose(rows, (1, 0, 2))[:, :, None, :]


def solution(mesh):
    placed = (
        P("rx", None, None, "tile", None, None),
        P(None, "tile", None),
        P("rx", None, None, None, "tile", None),
        P("rx", None),
        P(),
        P(),
    )
    return jax.shard_map(
        on_device,
        mesh=mesh,
        in_specs=placed,
        out_specs=P("rx", None, "tile", None),
        check_vma=False,
    )
```

```python
import functools

import jax
import jax.numpy as jnp
from jax import lax
from jax.experimental import pallas as pl
from jax.experimental.pallas import tpu as pltpu
from jax.sharding import PartitionSpec as P

XG = 8
RU = 4
MESSAGES = {3: (3,), 4: (4,)}
MESH = pl.DeviceIdType.MESH


def group_order(groups):
    far = groups // 2
    order = [far]
    for step in range(1, groups):
        for offset in (far - step, far + step):
            if 0 < offset < groups and offset not in order:
                order.append(offset)
    if 0 not in order:
        order.append(0)
    return order


def prepare_selection(place_ref, sel_ref, units):
    shape = sel_ref.shape
    row = lax.broadcasted_iota(jnp.int32, shape, 0)
    column = lax.broadcasted_iota(jnp.int32, shape, 1)
    capacity = place_ref.shape[1]
    slot = (row // (2 * capacity * XG)) * capacity + row % capacity
    wanted = jnp.zeros(shape, jnp.int32)
    for owner in range(place_ref.shape[0]):
        for number in range(capacity):
            wanted = jnp.where(slot == owner * capacity + number, place_ref[owner, number], wanted)
    same_x = (row // (2 * capacity)) % XG == column // (8 * units)
    same_part = (row // capacity) % 2 == (column // RU) % 2
    receiver = ((column // 8) % units) * RU + column % RU
    hit = same_x & same_part & (receiver == wanted)
    sel_ref[...] = jnp.where(hit, 1.0, 0.0).astype(jnp.bfloat16)


def prepare_coupling(index_ref, count_ref, weight_ref, coef_ref, own):
    owners, _, capacity = index_ref.shape
    sources, receivers = weight_ref.shape
    rows, columns = coef_ref.shape
    per_group = receivers // owners
    shape = (receivers, columns)
    column = lax.broadcasted_iota(jnp.int32, shape, 1)
    slot = (column // (2 * capacity * XG)) * capacity + column % capacity
    target = jnp.full(shape, -1, jnp.int32)
    for owner in range(owners):
        for number in range(capacity):
            used = number < count_ref[owner, own]
            listed = jnp.where(used, owner * per_group + index_ref[owner, own, number], -1)
            target = jnp.where(slot == owner * capacity + number, listed, target)
    hit = lax.broadcasted_iota(jnp.int32, shape, 0) == target
    chosen = jnp.where(hit, 1.0, 0.0).astype(jnp.bfloat16)
    weights = jnp.dot(weight_ref[...].astype(jnp.bfloat16), chosen, preferred_element_type=jnp.float32)
    block = rows // sources
    weights = jnp.broadcast_to(weights[None], (block, sources, columns)).reshape(rows, columns)
    row = lax.broadcasted_iota(jnp.int32, (rows, columns), 0)
    column = lax.broadcasted_iota(jnp.int32, (rows, columns), 1)
    same_x = row // (2 * sources) == (column // (2 * capacity)) % XG
    same_part = (row // sources) % 2 == (column // capacity) % 2
    coef_ref[...] = jnp.where(same_x & same_part, weights, 0.0).astype(jnp.bfloat16)


def kernel(messages, place_ref, index_ref, count_ref, h_ref, tx_ref, sigma_ref, weight_ref, out_ref,
           halo, sent, arrived, picked, fields, sel_ref, coef_ref, halo_send, halo_recv,
           tile_send, tile_recv, rx_send, rx_recv):
    tiles = lax.axis_size("tile")
    owners = lax.axis_size("rx")
    me = lax.axis_index("tile")
    own = lax.axis_index("rx")
    groups = tiles // XG
    order = group_order(groups)
    my_group = me // XG
    units = h_ref.shape[0]
    after = lax.rem(me + 1, tiles)

    barrier = pltpu.get_barrier_semaphore()

    def greet_tile(step, _):
        peer = lax.rem(me + step, tiles)
        pl.semaphore_signal(barrier, inc=1, device_id={"tile": peer}, device_id_type=MESH)
        return 0

    def greet_rx(step, _):
        peer = lax.rem(own + step, owners)
        pl.semaphore_signal(barrier, inc=1, device_id={"rx": peer}, device_id_type=MESH)
        return 0

    lax.fori_loop(1, tiles, greet_tile, 0)
    lax.fori_loop(1, owners, greet_rx, 0)
    pl.semaphore_wait(barrier, tiles + owners - 2)

    def halo_copy(unit):
        return pltpu.make_async_remote_copy(
            src_ref=h_ref.at[unit, pl.ds(1, 2)], dst_ref=halo.at[unit],
            send_sem=halo_send.at[unit], recv_sem=halo_recv.at[unit],
            device_id={"tile": after}, device_id_type=MESH)

    for unit in range(units):
        halo_copy(unit).start()

    inner = (me > 0).astype(jnp.float32)
    lanes = lax.broadcasted_iota(jnp.int32, (XG, 8, 128), 2)

    def lag_y(value):
        return jnp.where(lanes == 0, 0.0, pltpu.roll(value, 1, 2))

    def curl_block(unit, base):
        hx = h_ref[unit, 0, pl.ds(base, XG + 1)].astype(jnp.float32)
        hy = h_ref[unit, 1, pl.ds(base, XG + 1)].astype(jnp.float32)
        hz = h_ref[unit, 2, pl.ds(base + 1, XG)].astype(jnp.float32)
        py = halo[unit, 0, pl.ds(base, XG + 1)].astype(jnp.float32) * inner
        pz = halo[unit, 1, pl.ds(base + 1, XG)].astype(jnp.float32) * inner
        both_y = hy + py
        both_z = hz + pz
        diff_xy = hy - py
        curl_y = (hx[1:] - hx[:-1]) - (hz - pz)
        sum_x = hx[1:] + hx[:-1]
        average_x = 0.5 * ((both_z - lag_y(both_z)) - (both_y[1:] - both_y[:-1]))
        average_y = 0.5 * (curl_y + lag_y(curl_y))
        average_z = 0.5 * ((diff_xy[1:] + diff_xy[:-1]) - (sum_x - lag_y(sum_x)))
        sent[pl.ds(base, XG), unit, 0] = average_x.astype(jnp.bfloat16)
        sent[pl.ds(base, XG), unit, 1] = average_y.astype(jnp.bfloat16)
        sent[pl.ds(base, XG), unit, 2] = average_z.astype(jnp.bfloat16)

    first = 0
    for number, count in enumerate(messages):
        span = pl.ds(first, count)
        for unit in range(first, first + count):
            halo_copy(unit).wait_recv()
        for offset in order:
            base = lax.rem(my_group + offset, groups) * XG
            for unit in range(first, first + count):
                curl_block(unit, base)

            def send(step, _, base=base, span=span, number=number):
                layer = base + step

                @pl.when(layer != me)
                def _():
                    pltpu.make_async_remote_copy(
                        src_ref=sent.at[layer, span], dst_ref=arrived.at[me, span],
                        send_sem=tile_send.at[number],
                        recv_sem=tile_recv.at[number, my_group],
                        device_id={"tile": layer}, device_id_type=MESH).start()

                @pl.when(layer == me)
                def _():
                    pltpu.make_async_copy(
                        sent.at[layer, span], arrived.at[me, span],
                        tile_recv.at[number, my_group]).start()
                return 0

            lax.fori_loop(0, XG, send, 0)
        first += count

    prepare_selection(place_ref, sel_ref, units)
    prepare_coupling(index_ref, count_ref, weight_ref, coef_ref, own)

    def collect(offset):
        group = lax.rem(my_group + groups - offset, groups)
        first = 0
        for number, count in enumerate(messages):
            whole = arrived.at[pl.ds(group * XG, XG), pl.ds(first, count)]
            pltpu.make_async_copy(whole, whole, tile_recv.at[number, group]).wait()
            first += count
        for part in range(3):
            block = arrived[pl.ds(group * XG, XG), :, part]
            block = block.reshape(XG * units * 8, 128)
            chosen = jnp.dot(sel_ref[...], block, preferred_element_type=jnp.float32)
            picked[group, :, part] = chosen.astype(jnp.bfloat16).reshape(owners, 4 * XG, 128)
        fields[group, own] = picked[group, own]

        def forward(step, _):
            peer = lax.rem(own + step, owners)
            pltpu.make_async_remote_copy(
                src_ref=picked.at[group, peer], dst_ref=fields.at[group, own],
                send_sem=rx_send, recv_sem=rx_recv.at[group],
                device_id={"rx": peer}, device_id_type=MESH).start()
            return 0

        lax.fori_loop(1, owners, forward, 0)

    def finish(offset):
        group = lax.rem(my_group + groups - offset, groups)
        others = fields.at[group, pl.ds(0, owners - 1)]
        pltpu.make_async_copy(others, others, rx_recv.at[group]).wait()
        total = None
        for part in range(3):
            block = fields[group, :, part].reshape(owners * 4 * XG, 128)
            combined = jnp.dot(coef_ref[...], block, preferred_element_type=jnp.float32)
            term = combined * tx_ref[group, part].astype(jnp.float32)
            total = term if total is None else total + term
        total = total.reshape(XG, 2, out_ref.shape[2], 128)
        value = total[:, 0] - total[:, 1]
        out_ref[group] = value / sigma_ref[group][:, None, :]

    behind = 2 if groups > 2 else 1
    for place, offset in enumerate(order):
        collect(offset)
        if place >= behind:
            finish(order[place - behind])
    for offset in order[len(order) - min(behind, len(order)):]:
        finish(offset)

    for unit in range(units):
        halo_copy(unit).wait_send()
    first = 0
    for number, count in enumerate(messages):
        rest = sent.at[pl.ds(0, tiles - 1), pl.ds(first, count)]
        pltpu.make_async_copy(rest, rest, tile_send.at[number]).wait()
        first += count
    rest = picked.at[:, pl.ds(0, owners - 1)]
    pltpu.make_async_copy(rest, rest, rx_send).wait()


def transfer(place, index, count, h_units, tx_groups, sigma_groups, weight, messages, call_id):
    units = h_units.shape[0]
    groups, _, rows, cells_y = tx_groups.shape
    tiles = groups * XG
    owners, capacity = place.shape
    sources = rows // (2 * XG)
    smem = pl.BlockSpec(memory_space=pltpu.SMEM)
    vmem = pl.BlockSpec(memory_space=pltpu.VMEM)
    bf16 = jnp.bfloat16
    return pl.pallas_call(
        functools.partial(kernel, messages),
        out_shape=jax.ShapeDtypeStruct((groups, XG, sources, cells_y), jnp.float32),
        in_specs=[smem] * 3 + [vmem] * 4,
        out_specs=vmem,
        scratch_shapes=[
            pltpu.VMEM((units, 2, tiles + 1, 8, cells_y), bf16),
            pltpu.VMEM((tiles, units, 3, 8, cells_y), bf16),
            pltpu.VMEM((tiles, units, 3, 8, cells_y), bf16),
            pltpu.VMEM((groups, owners, 3, 4 * XG, cells_y), bf16),
            pltpu.VMEM((groups, owners, 3, 4 * XG, cells_y), bf16),
            pltpu.VMEM((owners * XG * 2 * capacity, XG * units * 8), bf16),
            pltpu.VMEM((rows, owners * XG * 2 * capacity), bf16),
            pltpu.SemaphoreType.DMA((units,)),
            pltpu.SemaphoreType.DMA((units,)),
            pltpu.SemaphoreType.DMA((len(messages),)),
            pltpu.SemaphoreType.DMA((len(messages), groups)),
            pltpu.SemaphoreType.DMA,
            pltpu.SemaphoreType.DMA((groups,)),
        ],
        compiler_params=pltpu.CompilerParams(
            collective_id=call_id, has_side_effects=True, vmem_limit_bytes=40 * 1024 * 1024),
    )(place, index, count, h_units, tx_groups, sigma_groups, weight)


def on_device(h_adjoint, conductivity, tx_field, data_weight, tow_index, tow_count):
    own = lax.axis_index("rx")
    receivers, parts, axes, _, layers, cells_y = h_adjoint.shape
    sources = tx_field.shape[0]
    owners, _, capacity = tow_index.shape
    groups = layers // XG

    tx_groups = tx_field.reshape(sources, parts, axes, groups, XG, cells_y)
    tx_groups = jnp.transpose(tx_groups, (3, 2, 4, 1, 0, 5))
    tx_groups = tx_groups.reshape(groups, axes, XG * parts * sources, cells_y)
    sigma_groups = conductivity.reshape(groups, XG, cells_y)

    number = jnp.arange(receivers, dtype=jnp.int32)
    used = jnp.arange(capacity, dtype=jnp.int32) < tow_count[:, :, None]
    slots = jnp.where(used, tow_index, -1).reshape(owners, owners * capacity)
    listed = jnp.any(slots[:, :, None] == number, axis=1)
    most = jnp.max(jnp.sum(listed.astype(jnp.int32), axis=1))

    mine = lax.dynamic_index_in_dim(slots, own, 0, False)
    before = jnp.any(mine[:, None, None] == number[:, None], axis=0) & (number[:, None] < number)
    rank = jnp.sum(before.astype(jnp.int32), axis=0)
    place = jnp.sum(jnp.where(mine[:, None] == number, rank, 0), axis=1).reshape(owners, capacity)
    has = jnp.any(mine[:, None] == number, axis=0)

    def exchange(units, call_id):
        if units * RU < receivers:
            order = jnp.arange(units * RU, dtype=jnp.int32)
            chosen = jnp.sum(jnp.where(has & (rank == order[:, None]), number, 0), axis=1)
            h_units = jnp.take(h_adjoint, chosen, axis=0, mode="clip")
            places = place
        else:
            h_units = h_adjoint
            places = lax.dynamic_index_in_dim(tow_index, own, 0, False)
        h_units = h_units.reshape(units, RU, parts, axes, layers, cells_y)
        h_units = jnp.transpose(h_units, (0, 3, 4, 2, 1, 5))
        h_units = h_units.reshape(units, axes, layers, parts * RU, cells_y)
        h_units = jnp.pad(h_units, ((0, 0), (0, 0), (1, 0), (0, 0), (0, 0)))
        return transfer(places, tow_index, tow_count, h_units, tx_groups, sigma_groups,
                        data_weight, MESSAGES[units], call_id)

    few, every = 3, receivers // RU
    rows = lax.cond(most <= few * RU, lambda: exchange(few, 0), lambda: exchange(every, 1))
    rows = rows.reshape(layers, sources, cells_y)
    return jnp.transpose(rows, (1, 0, 2))[:, :, None, :]


def solution(mesh):
    placed = (
        P("rx", None, None, "tile", None, None),
        P(None, "tile", None),
        P("rx", None, None, None, "tile", None),
        P("rx", None),
        P(),
        P(),
    )
    return jax.shard_map(
        on_device,
        mesh=mesh,
        in_specs=placed,
        out_specs=P("rx", None, "tile", None),
        check_vma=False,
    )
```

```python
import functools

import jax
import jax.numpy as jnp
from jax import lax
from jax.experimental import pallas as pl
from jax.experimental.pallas import tpu as pltpu
from jax.sharding import PartitionSpec as P

XG = 8
RU = 2
ROWS = 2 * RU
SIZES = (8, 10, 12)
MESH = pl.DeviceIdType.MESH


def group_order(groups):
    far = groups // 2
    order = [far]
    for step in range(1, groups):
        for offset in (far - step, far + step):
            if 0 < offset < groups and offset not in order:
                order.append(offset)
    if 0 not in order:
        order.append(0)
    return order


def prepare_selection(place_ref, sel_ref, units):
    shape = sel_ref.shape
    row = lax.broadcasted_iota(jnp.int32, shape, 0)
    column = lax.broadcasted_iota(jnp.int32, shape, 1)
    capacity = place_ref.shape[1]
    slot = (row // (2 * capacity * XG)) * capacity + row % capacity
    wanted = jnp.zeros(shape, jnp.int32)
    for owner in range(place_ref.shape[0]):
        for number in range(capacity):
            wanted = jnp.where(slot == owner * capacity + number, place_ref[owner, number], wanted)
    same_x = (row // (2 * capacity)) % XG == column // (ROWS * units)
    same_part = (row // capacity) % 2 == (column // RU) % 2
    receiver = ((column // ROWS) % units) * RU + column % RU
    hit = same_x & same_part & (receiver == wanted)
    sel_ref[...] = jnp.where(hit, 1.0, 0.0).astype(jnp.bfloat16)


def prepare_coupling(index_ref, count_ref, weight_ref, coef_ref, own):
    owners, _, capacity = index_ref.shape
    sources, receivers = weight_ref.shape
    rows, columns = coef_ref.shape
    per_group = receivers // owners
    shape = (receivers, columns)
    column = lax.broadcasted_iota(jnp.int32, shape, 1)
    slot = (column // (2 * capacity * XG)) * capacity + column % capacity
    target = jnp.full(shape, -1, jnp.int32)
    for owner in range(owners):
        for number in range(capacity):
            used = number < count_ref[owner, own]
            listed = jnp.where(used, owner * per_group + index_ref[owner, own, number], -1)
            target = jnp.where(slot == owner * capacity + number, listed, target)
    hit = lax.broadcasted_iota(jnp.int32, shape, 0) == target
    chosen = jnp.where(hit, 1.0, 0.0).astype(jnp.bfloat16)
    weights = jnp.dot(weight_ref[...].astype(jnp.bfloat16), chosen, preferred_element_type=jnp.float32)
    block = rows // sources
    weights = jnp.broadcast_to(weights[None], (block, sources, columns)).reshape(rows, columns)
    row = lax.broadcasted_iota(jnp.int32, (rows, columns), 0)
    column = lax.broadcasted_iota(jnp.int32, (rows, columns), 1)
    same_x = row // (2 * sources) == (column // (2 * capacity)) % XG
    same_part = (row // sources) % 2 == (column // capacity) % 2
    coef_ref[...] = jnp.where(same_x & same_part, weights, 0.0).astype(jnp.bfloat16)


def kernel(messages, place_ref, index_ref, count_ref, h_ref, tx_ref, sigma_ref, weight_ref, out_ref,
           halo, sent, arrived, picked, fields, sel_ref, coef_ref, halo_send, halo_recv,
           tile_send, tile_recv, rx_send, rx_recv):
    tiles = lax.axis_size("tile")
    owners = lax.axis_size("rx")
    me = lax.axis_index("tile")
    own = lax.axis_index("rx")
    groups = tiles // XG
    order = group_order(groups)
    my_group = me // XG
    units = h_ref.shape[0]
    after = lax.rem(me + 1, tiles)

    barrier = pltpu.get_barrier_semaphore()

    def greet_tile(step, _):
        peer = lax.rem(me + step, tiles)
        pl.semaphore_signal(barrier, inc=1, device_id={"tile": peer}, device_id_type=MESH)
        return 0

    def greet_rx(step, _):
        peer = lax.rem(own + step, owners)
        pl.semaphore_signal(barrier, inc=1, device_id={"rx": peer}, device_id_type=MESH)
        return 0

    lax.fori_loop(1, tiles, greet_tile, 0)
    lax.fori_loop(1, owners, greet_rx, 0)
    pl.semaphore_wait(barrier, tiles + owners - 2)

    def halo_copy(unit):
        return pltpu.make_async_remote_copy(
            src_ref=h_ref.at[unit, pl.ds(1, 2)], dst_ref=halo.at[unit],
            send_sem=halo_send.at[unit], recv_sem=halo_recv.at[unit],
            device_id={"tile": after}, device_id_type=MESH)

    for unit in range(units):
        halo_copy(unit).start()

    inner = (me > 0).astype(jnp.float32)
    lanes = lax.broadcasted_iota(jnp.int32, (XG, ROWS, 128), 2)

    def lag_y(value):
        return jnp.where(lanes == 0, 0.0, pltpu.roll(value, 1, 2))

    def curl_block(unit, base):
        hx = h_ref[unit, 0, pl.ds(base, XG + 1)].astype(jnp.float32)
        hy = h_ref[unit, 1, pl.ds(base, XG + 1)].astype(jnp.float32)
        hz = h_ref[unit, 2, pl.ds(base + 1, XG)].astype(jnp.float32)
        py = halo[unit, 0, pl.ds(base, XG + 1)].astype(jnp.float32) * inner
        pz = halo[unit, 1, pl.ds(base + 1, XG)].astype(jnp.float32) * inner
        both_y = hy + py
        both_z = hz + pz
        diff_xy = hy - py
        curl_y = (hx[1:] - hx[:-1]) - (hz - pz)
        sum_x = hx[1:] + hx[:-1]
        average_x = 0.5 * ((both_z - lag_y(both_z)) - (both_y[1:] - both_y[:-1]))
        average_y = 0.5 * (curl_y + lag_y(curl_y))
        average_z = 0.5 * ((diff_xy[1:] + diff_xy[:-1]) - (sum_x - lag_y(sum_x)))
        sent[pl.ds(base, XG), unit, 0] = average_x.astype(jnp.bfloat16)
        sent[pl.ds(base, XG), unit, 1] = average_y.astype(jnp.bfloat16)
        sent[pl.ds(base, XG), unit, 2] = average_z.astype(jnp.bfloat16)

    first = 0
    for number, count in enumerate(messages):
        span = pl.ds(first, count)
        for unit in range(first, first + count):
            halo_copy(unit).wait_recv()
        for offset in order:
            base = lax.rem(my_group + offset, groups) * XG
            for unit in range(first, first + count):
                curl_block(unit, base)

            def send(step, _, base=base, span=span, number=number):
                layer = base + step

                @pl.when(layer != me)
                def _():
                    pltpu.make_async_remote_copy(
                        src_ref=sent.at[layer, span], dst_ref=arrived.at[me, span],
                        send_sem=tile_send.at[number],
                        recv_sem=tile_recv.at[number, my_group],
                        device_id={"tile": layer}, device_id_type=MESH).start()

                @pl.when(layer == me)
                def _():
                    pltpu.make_async_copy(
                        sent.at[layer, span], arrived.at[me, span],
                        tile_recv.at[number, my_group]).start()
                return 0

            lax.fori_loop(0, XG, send, 0)
        first += count

    prepare_selection(place_ref, sel_ref, units)
    prepare_coupling(index_ref, count_ref, weight_ref, coef_ref, own)

    def collect(offset):
        group = lax.rem(my_group + groups - offset, groups)
        first = 0
        for number, count in enumerate(messages):
            whole = arrived.at[pl.ds(group * XG, XG), pl.ds(first, count)]
            pltpu.make_async_copy(whole, whole, tile_recv.at[number, group]).wait()
            first += count
        for part in range(3):
            block = arrived[pl.ds(group * XG, XG), :, part]
            block = block.reshape(XG * units * ROWS, 128)
            chosen = jnp.dot(sel_ref[...], block, preferred_element_type=jnp.float32)
            picked[group, :, part] = chosen.astype(jnp.bfloat16).reshape(owners, 4 * XG, 128)
        fields[group, own] = picked[group, own]

        def forward(step, _):
            peer = lax.rem(own + step, owners)
            pltpu.make_async_remote_copy(
                src_ref=picked.at[group, peer], dst_ref=fields.at[group, own],
                send_sem=rx_send, recv_sem=rx_recv.at[group],
                device_id={"rx": peer}, device_id_type=MESH).start()
            return 0

        lax.fori_loop(1, owners, forward, 0)

    def finish(offset):
        group = lax.rem(my_group + groups - offset, groups)
        others = fields.at[group, pl.ds(0, owners - 1)]
        pltpu.make_async_copy(others, others, rx_recv.at[group]).wait()
        total = None
        for part in range(3):
            block = fields[group, :, part].reshape(owners * 4 * XG, 128)
            combined = jnp.dot(coef_ref[...], block, preferred_element_type=jnp.float32)
            term = combined * tx_ref[group, part].astype(jnp.float32)
            total = term if total is None else total + term
        total = total.reshape(XG, 2, out_ref.shape[2], 128)
        value = total[:, 0] - total[:, 1]
        out_ref[group] = value / sigma_ref[group][:, None, :]

    behind = 2 if groups > 2 else 1
    for place, offset in enumerate(order):
        collect(offset)
        if place >= behind:
            finish(order[place - behind])
    for offset in order[len(order) - min(behind, len(order)):]:
        finish(offset)

    for unit in range(units):
        halo_copy(unit).wait_send()
    first = 0
    for number, count in enumerate(messages):
        rest = sent.at[pl.ds(0, tiles - 1), pl.ds(first, count)]
        pltpu.make_async_copy(rest, rest, tile_send.at[number]).wait()
        first += count
    rest = picked.at[:, pl.ds(0, owners - 1)]
    pltpu.make_async_copy(rest, rest, rx_send).wait()


def transfer(place, index, count, h_units, tx_groups, sigma_groups, weight, messages, call_id):
    units = h_units.shape[0]
    groups, _, rows, cells_y = tx_groups.shape
    tiles = groups * XG
    owners, capacity = place.shape
    sources = rows // (2 * XG)
    smem = pl.BlockSpec(memory_space=pltpu.SMEM)
    vmem = pl.BlockSpec(memory_space=pltpu.VMEM)
    bf16 = jnp.bfloat16
    return pl.pallas_call(
        functools.partial(kernel, messages),
        out_shape=jax.ShapeDtypeStruct((groups, XG, sources, cells_y), jnp.float32),
        in_specs=[smem] * 3 + [vmem] * 4,
        out_specs=vmem,
        scratch_shapes=[
            pltpu.VMEM((units, 2, tiles + 1, ROWS, cells_y), bf16),
            pltpu.VMEM((tiles, units, 3, ROWS, cells_y), bf16),
            pltpu.VMEM((tiles, units, 3, ROWS, cells_y), bf16),
            pltpu.VMEM((groups, owners, 3, 4 * XG, cells_y), bf16),
            pltpu.VMEM((groups, owners, 3, 4 * XG, cells_y), bf16),
            pltpu.VMEM((owners * XG * 2 * capacity, XG * units * ROWS), bf16),
            pltpu.VMEM((rows, owners * XG * 2 * capacity), bf16),
            pltpu.SemaphoreType.DMA((units,)),
            pltpu.SemaphoreType.DMA((units,)),
            pltpu.SemaphoreType.DMA((len(messages),)),
            pltpu.SemaphoreType.DMA((len(messages), groups)),
            pltpu.SemaphoreType.DMA,
            pltpu.SemaphoreType.DMA((groups,)),
        ],
        compiler_params=pltpu.CompilerParams(
            collective_id=call_id, has_side_effects=True, vmem_limit_bytes=40 * 1024 * 1024),
    )(place, index, count, h_units, tx_groups, sigma_groups, weight)


def on_device(h_adjoint, conductivity, tx_field, data_weight, tow_index, tow_count):
    own = lax.axis_index("rx")
    receivers, parts, axes, _, layers, cells_y = h_adjoint.shape
    sources = tx_field.shape[0]
    owners, _, capacity = tow_index.shape
    groups = layers // XG

    tx_groups = tx_field.reshape(sources, parts, axes, groups, XG, cells_y)
    tx_groups = jnp.transpose(tx_groups, (3, 2, 4, 1, 0, 5))
    tx_groups = tx_groups.reshape(groups, axes, XG * parts * sources, cells_y)
    sigma_groups = conductivity.reshape(groups, XG, cells_y)

    number = jnp.arange(receivers, dtype=jnp.int32)
    used = jnp.arange(capacity, dtype=jnp.int32) < tow_count[:, :, None]
    slots = jnp.where(used, tow_index, -1).reshape(owners, owners * capacity)
    listed = jnp.any(slots[:, :, None] == number, axis=1)
    most = jnp.max(jnp.sum(listed.astype(jnp.int32), axis=1))

    mine = lax.dynamic_index_in_dim(slots, own, 0, False)
    before = jnp.any(mine[:, None, None] == number[:, None], axis=0) & (number[:, None] < number)
    rank = jnp.sum(before.astype(jnp.int32), axis=0)
    place = jnp.sum(jnp.where(mine[:, None] == number, rank, 0), axis=1).reshape(owners, capacity)
    has = jnp.any(mine[:, None] == number, axis=0)

    def exchange(units, call_id):
        if units * RU < receivers:
            order = jnp.arange(units * RU, dtype=jnp.int32)
            chosen = jnp.sum(jnp.where(has & (rank == order[:, None]), number, 0), axis=1)
            h_units = jnp.take(h_adjoint, chosen, axis=0, mode="clip")
            places = place
        else:
            h_units = h_adjoint
            places = lax.dynamic_index_in_dim(tow_index, own, 0, False)
        h_units = h_units.reshape(units, RU, parts, axes, layers, cells_y)
        h_units = jnp.transpose(h_units, (0, 3, 4, 2, 1, 5))
        h_units = h_units.reshape(units, axes, layers, parts * RU, cells_y)
        h_units = jnp.pad(h_units, ((0, 0), (0, 0), (1, 0), (0, 0), (0, 0)))
        return transfer(places, tow_index, tow_count, h_units, tx_groups, sigma_groups,
                        data_weight, (units,), call_id)

    sizes = SIZES + (receivers,)
    size = sum((most > limit).astype(jnp.int32) for limit in SIZES)
    rows = lax.switch(size, [
        functools.partial(exchange, limit // RU, number) for number, limit in enumerate(sizes)])
    rows = rows.reshape(layers, sources, cells_y)
    return jnp.transpose(rows, (1, 0, 2))[:, :, None, :]


def solution(mesh):
    placed = (
        P("rx", None, None, "tile", None, None),
        P(None, "tile", None),
        P("rx", None, None, None, "tile", None),
        P("rx", None),
        P(),
        P(),
    )
    return jax.shard_map(
        on_device,
        mesh=mesh,
        in_specs=placed,
        out_specs=P("rx", None, "tile", None),
        check_vma=False,
    )
```

```python
import functools

import jax
import jax.numpy as jnp
from jax import lax
from jax.experimental import pallas as pl
from jax.experimental.pallas import tpu as pltpu
from jax.sharding import PartitionSpec as P

XG = 8
RU = 2
ROWS = 2 * RU
SIZES = (8, 10, 12)
MESH = pl.DeviceIdType.MESH


def group_order(groups):
    far = groups // 2
    order = [far]
    for step in range(1, groups):
        for offset in (far - step, far + step):
            if 0 < offset < groups and offset not in order:
                order.append(offset)
    if 0 not in order:
        order.append(0)
    return order


def before(mask, receivers, value):
    rank = jnp.zeros(value.shape, jnp.int32)
    for number in range(receivers):
        rank = rank + jnp.where(value > number, (mask >> number) & 1, 0)
    return rank


def prepare_rows(mask, rows_ref, h_ref, pick_ref):
    shape = pick_ref.shape
    axes, layers, width, cells_y = rows_ref.shape
    receivers = width // 2
    units = h_ref.shape[0]
    row = lax.broadcasted_iota(jnp.int32, shape, 0)
    column = lax.broadcasted_iota(jnp.int32, shape, 1)
    number = column % receivers
    wanted = (row // (ROWS * XG)) * RU + row % RU
    same_z = (row // ROWS) % XG == column // width
    same_part = (row // RU) % 2 == (column // receivers) % 2
    rank = before(mask, receivers, number)
    through = before(mask, receivers, number + 1)
    hit = same_z & same_part & (rank == wanted) & (through > rank)
    pick_ref[...] = jnp.where(hit, 1.0, 0.0).astype(jnp.bfloat16)
    h_ref[:, :, pl.ds(0, 1)] = jnp.zeros((units, axes, 1, ROWS, cells_y), jnp.bfloat16)

    def one(group, _):
        for axis in range(axes):
            block = rows_ref[axis, pl.ds(group * XG, XG)].reshape(XG * width, cells_y)
            chosen = jnp.dot(pick_ref[...], block, preferred_element_type=jnp.float32)
            chosen = chosen.astype(jnp.bfloat16).reshape(units, XG, ROWS, cells_y)
            h_ref[:, axis, pl.ds(1 + group * XG, XG)] = chosen
        return 0

    lax.fori_loop(0, layers // XG, one, 0)


def prepare_selection(mask, index_ref, sel_ref, units, own, owners, capacity, receivers):
    shape = sel_ref.shape
    row = lax.broadcasted_iota(jnp.int32, shape, 0)
    column = lax.broadcasted_iota(jnp.int32, shape, 1)
    slot = (row // (2 * capacity * XG)) * capacity + row % capacity
    wanted = jnp.zeros(shape, jnp.int32)
    for number in range(owners * capacity):
        wanted = jnp.where(slot == number, index_ref[own * (owners * capacity) + number], wanted)
    same_x = (row // (2 * capacity)) % XG == column // (ROWS * units)
    same_part = (row // capacity) % 2 == (column // RU) % 2
    place = ((column // ROWS) % units) * RU + column % RU
    hit = same_x & same_part & (place == before(mask, receivers, wanted))
    sel_ref[...] = jnp.where(hit, 1.0, 0.0).astype(jnp.bfloat16)


def prepare_source(tx_ref, source):
    sources, parts, axes, cells, _ = tx_ref.shape

    def one(number, _):
        for part in range(parts):
            row = pl.ds(part * sources + number, XG, stride=parts * sources)
            for axis in range(axes):
                field = tx_ref[number, part, axis].astype(jnp.float32)
                for group in range(cells // XG):
                    source[group, axis, row, :] = field[group * XG:(group + 1) * XG]
        return 0

    lax.fori_loop(0, sources, one, 0)


def prepare_coupling(index_ref, count_ref, weight_ref, coef_ref, own, owners, capacity):
    sources, receivers = weight_ref.shape
    rows, columns = coef_ref.shape
    per_group = receivers // owners
    shape = (receivers, columns)
    column = lax.broadcasted_iota(jnp.int32, shape, 1)
    slot = (column // (2 * capacity * XG)) * capacity + column % capacity
    target = jnp.full(shape, -1, jnp.int32)
    for owner in range(owners):
        for number in range(capacity):
            used = number < count_ref[owner, own]
            place = (owner * owners + own) * capacity + number
            listed = jnp.where(used, owner * per_group + index_ref[place], -1)
            target = jnp.where(slot == owner * capacity + number, listed, target)
    hit = lax.broadcasted_iota(jnp.int32, shape, 0) == target
    chosen = jnp.where(hit, 1.0, 0.0).astype(jnp.bfloat16)
    weights = jnp.dot(weight_ref[...].astype(jnp.bfloat16), chosen, preferred_element_type=jnp.float32)
    block = rows // sources
    weights = jnp.broadcast_to(weights[None], (block, sources, columns)).reshape(rows, columns)
    row = lax.broadcasted_iota(jnp.int32, (rows, columns), 0)
    column = lax.broadcasted_iota(jnp.int32, (rows, columns), 1)
    same_x = row // (2 * sources) == (column // (2 * capacity)) % XG
    same_part = (row // sources) % 2 == (column // capacity) % 2
    coef_ref[...] = jnp.where(same_x & same_part, weights, 0.0).astype(jnp.bfloat16)


def kernel(messages, mask_ref, index_ref, count_ref, rows_ref, tx_ref, sigma_ref, weight_ref, out_ref,
           h_ref, halo, sent, arrived, picked, fields, source, pick_ref, sel_ref, coef_ref, halo_send, halo_recv,
           tile_send, tile_recv, rx_send, rx_recv):
    tiles = lax.axis_size("tile")
    owners = lax.axis_size("rx")
    me = lax.axis_index("tile")
    own = lax.axis_index("rx")
    groups = tiles // XG
    order = group_order(groups)
    my_group = me // XG
    units = h_ref.shape[0]
    after = lax.rem(me + 1, tiles)

    barrier = pltpu.get_barrier_semaphore()

    def greet_tile(step, _):
        peer = lax.rem(me + step, tiles)
        pl.semaphore_signal(barrier, inc=1, device_id={"tile": peer}, device_id_type=MESH)
        return 0

    def greet_rx(step, _):
        peer = lax.rem(own + step, owners)
        pl.semaphore_signal(barrier, inc=1, device_id={"rx": peer}, device_id_type=MESH)
        return 0

    lax.fori_loop(1, tiles, greet_tile, 0)
    lax.fori_loop(1, owners, greet_rx, 0)
    mask = mask_ref[own]
    prepare_rows(mask, rows_ref, h_ref, pick_ref)
    pl.semaphore_wait(barrier, tiles + owners - 2)

    def halo_copy(unit):
        return pltpu.make_async_remote_copy(
            src_ref=h_ref.at[unit, pl.ds(1, 2)], dst_ref=halo.at[unit],
            send_sem=halo_send.at[unit], recv_sem=halo_recv.at[unit],
            device_id={"tile": after}, device_id_type=MESH)

    for unit in range(units):
        halo_copy(unit).start()

    inner = (me > 0).astype(jnp.float32)
    lanes = lax.broadcasted_iota(jnp.int32, (XG, ROWS, 128), 2)

    def lag_y(value):
        return jnp.where(lanes == 0, 0.0, pltpu.roll(value, 1, 2))

    def curl_block(unit, base):
        hx = h_ref[unit, 0, pl.ds(base, XG + 1)].astype(jnp.float32)
        hy = h_ref[unit, 1, pl.ds(base, XG + 1)].astype(jnp.float32)
        hz = h_ref[unit, 2, pl.ds(base + 1, XG)].astype(jnp.float32)
        py = halo[unit, 0, pl.ds(base, XG + 1)].astype(jnp.float32) * inner
        pz = halo[unit, 1, pl.ds(base + 1, XG)].astype(jnp.float32) * inner
        both_y = hy + py
        both_z = hz + pz
        diff_xy = hy - py
        curl_y = (hx[1:] - hx[:-1]) - (hz - pz)
        sum_x = hx[1:] + hx[:-1]
        average_x = 0.5 * ((both_z - lag_y(both_z)) - (both_y[1:] - both_y[:-1]))
        average_y = 0.5 * (curl_y + lag_y(curl_y))
        average_z = 0.5 * ((diff_xy[1:] + diff_xy[:-1]) - (sum_x - lag_y(sum_x)))
        sent[pl.ds(base, XG), unit, 0] = average_x.astype(jnp.bfloat16)
        sent[pl.ds(base, XG), unit, 1] = average_y.astype(jnp.bfloat16)
        sent[pl.ds(base, XG), unit, 2] = average_z.astype(jnp.bfloat16)

    first = 0
    for number, count in enumerate(messages):
        span = pl.ds(first, count)
        for unit in range(first, first + count):
            halo_copy(unit).wait_recv()
        for offset in order:
            base = lax.rem(my_group + offset, groups) * XG
            for unit in range(first, first + count):
                curl_block(unit, base)

            def send(step, _, base=base, span=span, number=number):
                layer = base + step

                @pl.when(layer != me)
                def _():
                    pltpu.make_async_remote_copy(
                        src_ref=sent.at[layer, span], dst_ref=arrived.at[me, span],
                        send_sem=tile_send.at[number],
                        recv_sem=tile_recv.at[number, my_group],
                        device_id={"tile": layer}, device_id_type=MESH).start()

                @pl.when(layer == me)
                def _():
                    pltpu.make_async_copy(
                        sent.at[layer, span], arrived.at[me, span],
                        tile_recv.at[number, my_group]).start()
                return 0

            lax.fori_loop(0, XG, send, 0)
        first += count

    prepare_source(tx_ref, source)
    capacity = index_ref.shape[0] // (owners * owners)
    receivers = rows_ref.shape[2] // 2
    prepare_selection(mask, index_ref, sel_ref, units, own, owners, capacity, receivers)
    prepare_coupling(index_ref, count_ref, weight_ref, coef_ref, own, owners, capacity)

    def collect(offset):
        group = lax.rem(my_group + groups - offset, groups)
        first = 0
        for number, count in enumerate(messages):
            whole = arrived.at[pl.ds(group * XG, XG), pl.ds(first, count)]
            pltpu.make_async_copy(whole, whole, tile_recv.at[number, group]).wait()
            first += count
        for part in range(3):
            block = arrived[pl.ds(group * XG, XG), :, part]
            block = block.reshape(XG * units * ROWS, 128)
            chosen = jnp.dot(sel_ref[...], block, preferred_element_type=jnp.float32)
            picked[group, :, part] = chosen.astype(jnp.bfloat16).reshape(owners, 4 * XG, 128)
        fields[group, own] = picked[group, own]

        def forward(step, _):
            peer = lax.rem(own + step, owners)
            pltpu.make_async_remote_copy(
                src_ref=picked.at[group, peer], dst_ref=fields.at[group, own],
                send_sem=rx_send, recv_sem=rx_recv.at[group],
                device_id={"rx": peer}, device_id_type=MESH).start()
            return 0

        lax.fori_loop(1, owners, forward, 0)

    def finish(offset):
        group = lax.rem(my_group + groups - offset, groups)
        others = fields.at[group, pl.ds(0, owners - 1)]
        pltpu.make_async_copy(others, others, rx_recv.at[group]).wait()
        total = None
        for part in range(3):
            block = fields[group, :, part].reshape(owners * 4 * XG, 128)
            combined = jnp.dot(coef_ref[...], block, preferred_element_type=jnp.float32)
            term = combined * source[group, part]
            total = term if total is None else total + term
        sources = tx_ref.shape[0]
        total = total.reshape(XG, 2, sources, 128)
        value = (total[:, 0] - total[:, 1]) / sigma_ref[group][:, None, :]
        for step in range(XG):
            out_ref[pl.ds(group * XG + step, sources, stride=tiles), :] = value[step]

    behind = 2 if groups > 2 else 1
    for place, offset in enumerate(order):
        collect(offset)
        if place >= behind:
            finish(order[place - behind])
    for offset in order[len(order) - min(behind, len(order)):]:
        finish(offset)

    for unit in range(units):
        halo_copy(unit).wait_send()
    first = 0
    for number, count in enumerate(messages):
        rest = sent.at[pl.ds(0, tiles - 1), pl.ds(first, count)]
        pltpu.make_async_copy(rest, rest, tile_send.at[number]).wait()
        first += count
    rest = picked.at[:, pl.ds(0, owners - 1)]
    pltpu.make_async_copy(rest, rest, rx_send).wait()


def transfer(mask, index, count, h_rows, tx_rows, sigma_groups, weight, units, call_id):
    sources, parts, axes, tiles, cells_y = tx_rows.shape
    groups = tiles // XG
    owners = count.shape[0]
    capacity = index.shape[0] // (owners * owners)
    width = h_rows.shape[2]
    rows = XG * parts * sources
    smem = pl.BlockSpec(memory_space=pltpu.SMEM)
    vmem = pl.BlockSpec(memory_space=pltpu.VMEM)
    bf16 = jnp.bfloat16
    return pl.pallas_call(
        functools.partial(kernel, (units,)),
        out_shape=jax.ShapeDtypeStruct((sources * tiles, cells_y), jnp.float32),
        in_specs=[smem] * 3 + [vmem] * 4,
        out_specs=vmem,
        scratch_shapes=[
            pltpu.VMEM((units, axes, tiles + 1, ROWS, cells_y), bf16),
            pltpu.VMEM((units, 2, tiles + 1, ROWS, cells_y), bf16),
            pltpu.VMEM((tiles, units, 3, ROWS, cells_y), bf16),
            pltpu.VMEM((tiles, units, 3, ROWS, cells_y), bf16),
            pltpu.VMEM((groups, owners, 3, 4 * XG, cells_y), bf16),
            pltpu.VMEM((groups, owners, 3, 4 * XG, cells_y), bf16),
            pltpu.VMEM((groups, axes, rows, cells_y), jnp.float32),
            pltpu.VMEM((units * XG * ROWS, XG * width), bf16),
            pltpu.VMEM((owners * XG * 2 * capacity, XG * units * ROWS), bf16),
            pltpu.VMEM((rows, owners * XG * 2 * capacity), bf16),
            pltpu.SemaphoreType.DMA((units,)),
            pltpu.SemaphoreType.DMA((units,)),
            pltpu.SemaphoreType.DMA((1,)),
            pltpu.SemaphoreType.DMA((1, groups)),
            pltpu.SemaphoreType.DMA,
            pltpu.SemaphoreType.DMA((groups,)),
        ],
        compiler_params=pltpu.CompilerParams(
            collective_id=call_id, has_side_effects=True, vmem_limit_bytes=40 * 1024 * 1024),
    )(mask, index, count, h_rows, tx_rows, sigma_groups, weight)


def on_device(h_adjoint, conductivity, tx_field, data_weight, tow_index, tow_count):
    receivers, parts, axes, _, layers, cells_y = h_adjoint.shape
    sources = tx_field.shape[0]
    capacity = tow_index.shape[2]
    groups = layers // XG

    tx_rows = tx_field.reshape(sources, parts, axes, layers, cells_y)
    sigma_groups = conductivity.reshape(groups, XG, cells_y)

    h_rows = h_adjoint.reshape(receivers, parts, axes, layers, cells_y)
    h_rows = jnp.transpose(h_rows, (2, 3, 1, 0, 4)).reshape(axes, layers, parts * receivers, cells_y)

    used = jnp.arange(capacity, dtype=jnp.int32) < tow_count[:, :, None]
    bits = jnp.where(used, jnp.int32(1) << tow_index, 0)
    mask = lax.reduce(bits, jnp.int32(0), lax.bitwise_or, (1, 2))
    most = jnp.max(lax.population_count(mask))

    def exchange(size, call_id):
        return transfer(mask, tow_index.reshape(-1), tow_count, h_rows, tx_rows, sigma_groups,
                        data_weight, size // RU, call_id)

    sizes = SIZES + (receivers,)
    size = sum((most > limit).astype(jnp.int32) for limit in SIZES)
    rows = lax.switch(size, [
        functools.partial(exchange, limit, number) for number, limit in enumerate(sizes)])
    return rows.reshape(sources, layers, 1, cells_y)


def solution(mesh):
    placed = (
        P("rx", None, None, "tile", None, None),
        P(None, "tile", None),
        P("rx", None, None, None, "tile", None),
        P("rx", None),
        P(),
        P(),
    )
    return jax.shard_map(
        on_device,
        mesh=mesh,
        in_specs=placed,
        out_specs=P("rx", None, "tile", None),
        check_vma=False,
    )
```

```python
import functools

import jax
import jax.numpy as jnp
from jax import lax
from jax.experimental import pallas as pl
from jax.experimental.pallas import tpu as pltpu
from jax.sharding import PartitionSpec as P

XG = 8
RU = 1
ROWS = 2 * RU
SIZES = (8, 9, 10, 12)
MESH = pl.DeviceIdType.MESH


def group_order(groups):
    far = groups // 2
    order = [far]
    for step in range(1, groups):
        for offset in (far - step, far + step):
            if 0 < offset < groups and offset not in order:
                order.append(offset)
    if 0 not in order:
        order.append(0)
    return order


def before(mask, receivers, value):
    rank = jnp.zeros(value.shape, jnp.int32)
    for number in range(receivers):
        rank = rank + jnp.where(value > number, (mask >> number) & 1, 0)
    return rank


def prepare_rows(mask, rows_ref, h_ref, pick_ref):
    shape = pick_ref.shape
    axes, layers, width, cells_y = rows_ref.shape
    receivers = width // 2
    units = h_ref.shape[0]
    row = lax.broadcasted_iota(jnp.int32, shape, 0)
    column = lax.broadcasted_iota(jnp.int32, shape, 1)
    number = column % receivers
    wanted = (row // (ROWS * XG)) * RU + row % RU
    same_z = (row // ROWS) % XG == column // width
    same_part = (row // RU) % 2 == (column // receivers) % 2
    rank = before(mask, receivers, number)
    through = before(mask, receivers, number + 1)
    hit = same_z & same_part & (rank == wanted) & (through > rank)
    pick_ref[...] = jnp.where(hit, 1.0, 0.0).astype(jnp.bfloat16)
    h_ref[:, :, pl.ds(0, 1)] = jnp.zeros((units, axes, 1, ROWS, cells_y), jnp.bfloat16)

    def one(group, _):
        for axis in range(axes):
            block = rows_ref[axis, pl.ds(group * XG, XG)].reshape(XG * width, cells_y)
            chosen = jnp.dot(pick_ref[...], block, preferred_element_type=jnp.float32)
            chosen = chosen.astype(jnp.bfloat16).reshape(units, XG, ROWS, cells_y)
            h_ref[:, axis, pl.ds(1 + group * XG, XG)] = chosen
        return 0

    lax.fori_loop(0, layers // XG, one, 0)


def prepare_selection(mask, index_ref, sel_ref, units, own, owners, capacity, receivers):
    shape = sel_ref.shape
    row = lax.broadcasted_iota(jnp.int32, shape, 0)
    column = lax.broadcasted_iota(jnp.int32, shape, 1)
    slot = (row // (2 * capacity * XG)) * capacity + row % capacity
    wanted = jnp.zeros(shape, jnp.int32)
    for number in range(owners * capacity):
        wanted = jnp.where(slot == number, index_ref[own * (owners * capacity) + number], wanted)
    same_x = (row // (2 * capacity)) % XG == column // (ROWS * units)
    same_part = (row // capacity) % 2 == (column // RU) % 2
    place = ((column // ROWS) % units) * RU + column % RU
    hit = same_x & same_part & (place == before(mask, receivers, wanted))
    sel_ref[...] = jnp.where(hit, 1.0, 0.0).astype(jnp.bfloat16)


def prepare_source(tx_ref, source):
    sources, parts, axes, cells, _ = tx_ref.shape

    def one(number, _):
        for part in range(parts):
            row = pl.ds(part * sources + number, XG, stride=parts * sources)
            for axis in range(axes):
                field = tx_ref[number, part, axis].astype(jnp.float32)
                for group in range(cells // XG):
                    source[group, axis, row, :] = field[group * XG:(group + 1) * XG]
        return 0

    lax.fori_loop(0, sources, one, 0)


def prepare_coupling(index_ref, count_ref, weight_ref, coef_ref, own, owners, capacity):
    sources, receivers = weight_ref.shape
    rows, columns = coef_ref.shape
    per_group = receivers // owners
    shape = (receivers, columns)
    column = lax.broadcasted_iota(jnp.int32, shape, 1)
    slot = (column // (2 * capacity * XG)) * capacity + column % capacity
    target = jnp.full(shape, -1, jnp.int32)
    for owner in range(owners):
        for number in range(capacity):
            used = number < count_ref[owner, own]
            place = (owner * owners + own) * capacity + number
            listed = jnp.where(used, owner * per_group + index_ref[place], -1)
            target = jnp.where(slot == owner * capacity + number, listed, target)
    hit = lax.broadcasted_iota(jnp.int32, shape, 0) == target
    chosen = jnp.where(hit, 1.0, 0.0).astype(jnp.bfloat16)
    weights = jnp.dot(weight_ref[...].astype(jnp.bfloat16), chosen, preferred_element_type=jnp.float32)
    block = rows // sources
    weights = jnp.broadcast_to(weights[None], (block, sources, columns)).reshape(rows, columns)
    row = lax.broadcasted_iota(jnp.int32, (rows, columns), 0)
    column = lax.broadcasted_iota(jnp.int32, (rows, columns), 1)
    same_x = row // (2 * sources) == (column // (2 * capacity)) % XG
    same_part = (row // sources) % 2 == (column // capacity) % 2
    coef_ref[...] = jnp.where(same_x & same_part, weights, 0.0).astype(jnp.bfloat16)


def kernel(messages, mask_ref, index_ref, count_ref, rows_ref, tx_ref, sigma_ref, weight_ref, out_ref,
           h_ref, halo, sent, arrived, picked, fields, source, pick_ref, sel_ref, coef_ref, halo_send, halo_recv,
           tile_send, tile_recv, rx_send, rx_recv):
    tiles = lax.axis_size("tile")
    owners = lax.axis_size("rx")
    me = lax.axis_index("tile")
    own = lax.axis_index("rx")
    groups = tiles // XG
    order = group_order(groups)
    my_group = me // XG
    units = h_ref.shape[0]
    after = lax.rem(me + 1, tiles)

    barrier = pltpu.get_barrier_semaphore()

    def greet_tile(step, _):
        peer = lax.rem(me + step, tiles)
        pl.semaphore_signal(barrier, inc=1, device_id={"tile": peer}, device_id_type=MESH)
        return 0

    def greet_rx(step, _):
        peer = lax.rem(own + step, owners)
        pl.semaphore_signal(barrier, inc=1, device_id={"rx": peer}, device_id_type=MESH)
        return 0

    lax.fori_loop(1, tiles, greet_tile, 0)
    lax.fori_loop(1, owners, greet_rx, 0)
    mask = mask_ref[own]
    prepare_rows(mask, rows_ref, h_ref, pick_ref)
    pl.semaphore_wait(barrier, tiles + owners - 2)

    def halo_copy(unit):
        return pltpu.make_async_remote_copy(
            src_ref=h_ref.at[unit, pl.ds(1, 2)], dst_ref=halo.at[unit],
            send_sem=halo_send.at[unit], recv_sem=halo_recv.at[unit],
            device_id={"tile": after}, device_id_type=MESH)

    for unit in range(units):
        halo_copy(unit).start()

    inner = (me > 0).astype(jnp.float32)
    lanes = lax.broadcasted_iota(jnp.int32, (XG, ROWS, 128), 2)

    def lag_y(value):
        return jnp.where(lanes == 0, 0.0, pltpu.roll(value, 1, 2))

    def curl_block(unit, base):
        hx = h_ref[unit, 0, pl.ds(base, XG + 1)].astype(jnp.float32)
        hy = h_ref[unit, 1, pl.ds(base, XG + 1)].astype(jnp.float32)
        hz = h_ref[unit, 2, pl.ds(base + 1, XG)].astype(jnp.float32)
        py = halo[unit, 0, pl.ds(base, XG + 1)].astype(jnp.float32) * inner
        pz = halo[unit, 1, pl.ds(base + 1, XG)].astype(jnp.float32) * inner
        both_y = hy + py
        both_z = hz + pz
        diff_xy = hy - py
        curl_y = (hx[1:] - hx[:-1]) - (hz - pz)
        sum_x = hx[1:] + hx[:-1]
        average_x = 0.5 * ((both_z - lag_y(both_z)) - (both_y[1:] - both_y[:-1]))
        average_y = 0.5 * (curl_y + lag_y(curl_y))
        average_z = 0.5 * ((diff_xy[1:] + diff_xy[:-1]) - (sum_x - lag_y(sum_x)))
        sent[pl.ds(base, XG), unit, 0] = average_x.astype(jnp.bfloat16)
        sent[pl.ds(base, XG), unit, 1] = average_y.astype(jnp.bfloat16)
        sent[pl.ds(base, XG), unit, 2] = average_z.astype(jnp.bfloat16)

    first = 0
    for number, count in enumerate(messages):
        span = pl.ds(first, count)
        for unit in range(first, first + count):
            halo_copy(unit).wait_recv()
        for offset in order:
            base = lax.rem(my_group + offset, groups) * XG
            for unit in range(first, first + count):
                curl_block(unit, base)

            def send(step, _, base=base, span=span, number=number):
                layer = base + step

                @pl.when(layer != me)
                def _():
                    pltpu.make_async_remote_copy(
                        src_ref=sent.at[layer, span], dst_ref=arrived.at[me, span],
                        send_sem=tile_send.at[number],
                        recv_sem=tile_recv.at[number, my_group],
                        device_id={"tile": layer}, device_id_type=MESH).start()

                @pl.when(layer == me)
                def _():
                    pltpu.make_async_copy(
                        sent.at[layer, span], arrived.at[me, span],
                        tile_recv.at[number, my_group]).start()
                return 0

            lax.fori_loop(0, XG, send, 0)
        first += count

    prepare_source(tx_ref, source)
    capacity = index_ref.shape[0] // (owners * owners)
    receivers = rows_ref.shape[2] // 2
    prepare_selection(mask, index_ref, sel_ref, units, own, owners, capacity, receivers)
    prepare_coupling(index_ref, count_ref, weight_ref, coef_ref, own, owners, capacity)

    def collect(offset):
        group = lax.rem(my_group + groups - offset, groups)
        first = 0
        for number, count in enumerate(messages):
            whole = arrived.at[pl.ds(group * XG, XG), pl.ds(first, count)]
            pltpu.make_async_copy(whole, whole, tile_recv.at[number, group]).wait()
            first += count
        for part in range(3):
            block = arrived[pl.ds(group * XG, XG), :, part]
            block = block.reshape(XG * units * ROWS, 128)
            chosen = jnp.dot(sel_ref[...], block, preferred_element_type=jnp.float32)
            picked[group, :, part] = chosen.astype(jnp.bfloat16).reshape(owners, 4 * XG, 128)
        fields[group, own] = picked[group, own]

        def forward(step, _):
            peer = lax.rem(own + step, owners)
            pltpu.make_async_remote_copy(
                src_ref=picked.at[group, peer], dst_ref=fields.at[group, own],
                send_sem=rx_send, recv_sem=rx_recv.at[group],
                device_id={"rx": peer}, device_id_type=MESH).start()
            return 0

        lax.fori_loop(1, owners, forward, 0)

    def finish(offset):
        group = lax.rem(my_group + groups - offset, groups)
        others = fields.at[group, pl.ds(0, owners - 1)]
        pltpu.make_async_copy(others, others, rx_recv.at[group]).wait()
        total = None
        for part in range(3):
            block = fields[group, :, part].reshape(owners * 4 * XG, 128)
            combined = jnp.dot(coef_ref[...], block, preferred_element_type=jnp.float32)
            term = combined * source[group, part]
            total = term if total is None else total + term
        sources = tx_ref.shape[0]
        total = total.reshape(XG, 2, sources, 128)
        value = (total[:, 0] - total[:, 1]) / sigma_ref[group][:, None, :]
        for step in range(XG):
            out_ref[pl.ds(group * XG + step, sources, stride=tiles), :] = value[step]

    behind = 2 if groups > 2 else 1
    for place, offset in enumerate(order):
        collect(offset)
        if place >= behind:
            finish(order[place - behind])
    for offset in order[len(order) - min(behind, len(order)):]:
        finish(offset)

    for unit in range(units):
        halo_copy(unit).wait_send()
    first = 0
    for number, count in enumerate(messages):
        rest = sent.at[pl.ds(0, tiles - 1), pl.ds(first, count)]
        pltpu.make_async_copy(rest, rest, tile_send.at[number]).wait()
        first += count
    rest = picked.at[:, pl.ds(0, owners - 1)]
    pltpu.make_async_copy(rest, rest, rx_send).wait()


def transfer(mask, index, count, h_rows, tx_rows, sigma_groups, weight, units, call_id):
    sources, parts, axes, tiles, cells_y = tx_rows.shape
    groups = tiles // XG
    owners = count.shape[0]
    capacity = index.shape[0] // (owners * owners)
    width = h_rows.shape[2]
    rows = XG * parts * sources
    smem = pl.BlockSpec(memory_space=pltpu.SMEM)
    vmem = pl.BlockSpec(memory_space=pltpu.VMEM)
    bf16 = jnp.bfloat16
    return pl.pallas_call(
        functools.partial(kernel, (units,)),
        out_shape=jax.ShapeDtypeStruct((sources * tiles, cells_y), jnp.float32),
        in_specs=[smem] * 3 + [vmem] * 4,
        out_specs=vmem,
        scratch_shapes=[
            pltpu.VMEM((units, axes, tiles + 1, ROWS, cells_y), bf16),
            pltpu.VMEM((units, 2, tiles + 1, ROWS, cells_y), bf16),
            pltpu.VMEM((tiles, units, 3, ROWS, cells_y), bf16),
            pltpu.VMEM((tiles, units, 3, ROWS, cells_y), bf16),
            pltpu.VMEM((groups, owners, 3, 4 * XG, cells_y), bf16),
            pltpu.VMEM((groups, owners, 3, 4 * XG, cells_y), bf16),
            pltpu.VMEM((groups, axes, rows, cells_y), jnp.float32),
            pltpu.VMEM((units * XG * ROWS, XG * width), bf16),
            pltpu.VMEM((owners * XG * 2 * capacity, XG * units * ROWS), bf16),
            pltpu.VMEM((rows, owners * XG * 2 * capacity), bf16),
            pltpu.SemaphoreType.DMA((units,)),
            pltpu.SemaphoreType.DMA((units,)),
            pltpu.SemaphoreType.DMA((1,)),
            pltpu.SemaphoreType.DMA((1, groups)),
            pltpu.SemaphoreType.DMA,
            pltpu.SemaphoreType.DMA((groups,)),
        ],
        compiler_params=pltpu.CompilerParams(
            collective_id=call_id, has_side_effects=True, vmem_limit_bytes=40 * 1024 * 1024),
    )(mask, index, count, h_rows, tx_rows, sigma_groups, weight)


def on_device(h_adjoint, conductivity, tx_field, data_weight, tow_index, tow_count):
    receivers, parts, axes, _, layers, cells_y = h_adjoint.shape
    sources = tx_field.shape[0]
    capacity = tow_index.shape[2]
    groups = layers // XG

    tx_rows = tx_field.reshape(sources, parts, axes, layers, cells_y)
    sigma_groups = conductivity.reshape(groups, XG, cells_y)

    h_rows = h_adjoint.reshape(receivers, parts, axes, layers, cells_y)
    h_rows = jnp.transpose(h_rows, (2, 3, 1, 0, 4)).reshape(axes, layers, parts * receivers, cells_y)

    used = jnp.arange(capacity, dtype=jnp.int32) < tow_count[:, :, None]
    bits = jnp.where(used, jnp.int32(1) << tow_index, 0)
    mask = lax.reduce(bits, jnp.int32(0), lax.bitwise_or, (1, 2))
    most = jnp.max(lax.population_count(mask))

    def exchange(size, call_id):
        return transfer(mask, tow_index.reshape(-1), tow_count, h_rows, tx_rows, sigma_groups,
                        data_weight, size // RU, call_id)

    sizes = SIZES + (receivers,)
    size = sum((most > limit).astype(jnp.int32) for limit in SIZES)
    rows = lax.switch(size, [
        functools.partial(exchange, limit, number) for number, limit in enumerate(sizes)])
    return rows.reshape(sources, layers, 1, cells_y)


def solution(mesh):
    placed = (
        P("rx", None, None, "tile", None, None),
        P(None, "tile", None),
        P("rx", None, None, None, "tile", None),
        P("rx", None),
        P(),
        P(),
    )
    return jax.shard_map(
        on_device,
        mesh=mesh,
        in_specs=placed,
        out_specs=P("rx", None, "tile", None),
        check_vma=False,
    )
```
